128 devices in a mesh: req: 64 (over z, y, x_hi, core), tp: 2 (over x_lo).
Axes of the slice: x: 4 (x_hi: 2, x_lo: 2; x = x_hi * 2 + x_lo), y: 4, z: 4, core: 2. Of those that a mesh axis runs over, the one named last changes fastest.
Arguments:
- arrivals: bfloat16 [32768, 2048], P('req', 'tp'), may hold values from -16 to 16
- packing: int32 [256], P('req'), may hold values from 0 to 255, as said below
- segment_ids: int32 [32768], P('req'), may hold values from 0 to 32767, as said below
- page_table: int32 [256], P('req'), may hold values from 0 to 255, as said below
- attn_gain: float32 [2048], replicated, may hold values from 0.25 to 1.75
- w_query: bfloat16 [2048, 2048], P(None, 'tp'), may hold values from -0.015625 to 0.015625
- w_key: bfloat16 [2048, 2048], P(None, 'tp'), may hold values from -0.125 to 0.125
- w_value: bfloat16 [2048, 2048], P(None, 'tp'), may hold values from -0.125 to 0.125
- w_out: bfloat16 [2048, 2048], P('tp'), may hold values from -0.1875 to 0.1875
- rel_bias: float32 [32, 32], P(None, 'tp'), may hold values from -4 to 260
- final_gain: float32 [2048], replicated, may hold values from 0.25 to 1.75
- cross_key: bfloat16 [2048, 2048], P(None, 'tp'), may hold values from -0.125 to 0.125
- cross_value: bfloat16 [2048, 2048], P(None, 'tp'), may hold values from -0.125 to 0.125
Outputs:
- hidden: bfloat16 [32768, 2048], P('req', 'tp')
- cache: bfloat16 [256, 128, 2, 2048], P('req', None, None, 'tp')
The draws below stay inside these ranges and needn't reach their ends.
Inputs may be any that keep to these rules, and one draw needn't show every extreme that they name: `packing`: A permutation of the block numbers; the entries of index r of req name, by their quotient by 4, the indices r XOR m for every m below 4, each exactly 1 times. `segment_ids`: Non-decreasing; every segment lies within the 512 tokens of one index of req and has at most 256 tokens; some index holds one of exactly 256. `page_table`: A permutation of the slots; the entries of index r of req name, by their quotient by 4, the indices r XOR m for every m below 4, each exactly 1 times; slot s lies on index s // 4 of req.
All inputs are finite; a program needn't handle non-finite values.
Results may differ from the reference program's by a relative error of at most 0.01.
Values may be sent and summed in bfloat16 or wider, within the bound.
No kernel may reach another device: no remote copies, remote signals or barrier semaphores. Data moves between devices by JAX's collectives and lax.ppermute only.
A program may use at most 256 MiB of HBM per device.

```python
import jax
import jax.numpy as jnp
from jax import lax

D = 2048
HEADS = 32
HEAD_DIM = 64
BUCKETS = 32
PAGE = 128
TOK_DEV = 512
INNER = 2048
HEAD_GROUPS = 2
LONG = 256
N_REQ = 64


def owner_slots(key_base, per_device, devices):
    group_size = min(per_device, devices)
    capacity = per_device // group_size
    key_a, key_b = jax.random.split(key_base, 2)
    lane_order = jax.vmap(lambda subkey: jax.random.permutation(subkey, per_device))(jax.random.split(key_a, devices)).astype(jnp.int32)
    arrangement = jax.vmap(lambda subkey: jax.random.permutation(subkey, per_device))(jax.random.split(key_b, devices)).astype(jnp.int32)
    sender = jnp.arange(devices, dtype=jnp.int32)[:, None]
    offset_bits = lane_order // capacity
    owners = jnp.bitwise_xor(sender, offset_bits).astype(jnp.int32)
    slots = owners * per_device + arrangement[owners, lane_order]
    return slots.reshape(-1).astype(jnp.int32)


def draw_packing(key, part):
    return owner_slots(jax.random.fold_in(key, 11), TOK_DEV // PAGE, N_REQ)


def draw_page_table(key, part):
    return owner_slots(jax.random.fold_in(key, 23), TOK_DEV // PAGE, N_REQ)


def draw_segment_ids(key, part):
    key_a, key_b = jax.random.split(jax.random.fold_in(key, 37))
    position = jnp.arange(TOK_DEV, dtype=jnp.int32)[None, :]
    device = jnp.arange(N_REQ, dtype=jnp.int32)[:, None]
    starts = jax.random.randint(key_a, (N_REQ, TOK_DEV), 0, 32) == 0
    starts = starts | (position % (LONG // 4) == 0)
    rotation = jax.random.randint(key_b, (), 0, 4)
    holder = (device + rotation) % 4 == 0
    starts = jnp.where(holder & (position < LONG), position == 0, starts)
    starts = starts | holder & (position == LONG)
    numbers = jnp.cumsum(starts.astype(jnp.int32), axis=1) - 1 + device * TOK_DEV
    return numbers.reshape(-1).astype(jnp.int32)


def draw_arrivals(key, part):
    key_a, key_b = jax.random.split(jax.random.fold_in(key, 41), 2)
    row_count = TOK_DEV * N_REQ
    column = jnp.arange(D, dtype=jnp.float32) / (D - 1)
    row_scale = 0.3 * 10.0 ** jax.random.uniform(key_b, (row_count, 1), jnp.float32, 0.0, 1.0)
    base = jnp.clip(jax.random.normal(key_a, (row_count, D), jnp.float32), -4.0, 4.0)
    column_scale = 3.0 ** (0.5 * column)
    return jnp.clip(base * row_scale * column_scale[None, :], -16.0, 16.0).astype(jnp.bfloat16)


def draw_rel_bias(key, part):
    key_a = jax.random.fold_in(jax.random.fold_in(key, 51), 0)
    return jnp.clip(jax.random.normal(key_a, (BUCKETS, HEADS), jnp.float32), -4.0, 4.0)


def raised(entries, own_key, source, target, blocks, factor):
    def block_of(axis_at):
        return (jnp.arange(entries.shape[axis_at]) // (entries.shape[axis_at] // blocks)).reshape((-1,) + (1,) * (entries.ndim - 1 - axis_at))

    near = jax.random.permutation(own_key, blocks)[block_of(target)]
    other_side = (block_of(target) + blocks // 2) % blocks
    return jnp.where((block_of(source) == near) | (block_of(source) == other_side), factor * entries, entries)


def levels(stream_key, shape, cuts, least, top_value):
    factor_of = 1.0
    for dim, shards_of in cuts:
        heights = jax.random.uniform(jax.random.fold_in(jax.random.fold_in(stream_key, 6), dim), (shards_of,), jnp.float32, least / len(cuts), top_value / len(cuts))
        factor_of = factor_of * jnp.repeat(jnp.exp(heights), shape[dim] // shards_of).reshape((-1,) + (1,) * (len(shape) - 1 - dim))
    return factor_of


def scatter_about(key, extent, spread, most, cuts=(), kind=jnp.bfloat16):
    result = spread * jax.random.normal(key, extent, jnp.float32)
    if cuts:
        result = result * levels(key, extent, cuts, -0.22, 0.18)
    return jnp.clip(result, -most, most).astype(kind)


def noise_with(own_key, extent, scale, most, cuts, heavy, kind=jnp.bfloat16):
    values = scale * jax.random.normal(own_key, extent, jnp.float32)
    if cuts:
        values = values * levels(own_key, extent, cuts, -0.22, 0.18)
    return jnp.clip(raised(values, jax.random.fold_in(own_key, 3), *heavy), -most, most).astype(kind)


def setup_inputs(seed: int = 0) -> dict:
    keys = jax.random.split(jax.random.key(seed), 14)
    return {
        "arrivals": draw_arrivals(jax.random.fold_in(keys[13], 71), 0),
        "packing": draw_packing(jax.random.fold_in(keys[13], 71), 0),
        "segment_ids": draw_segment_ids(jax.random.fold_in(keys[13], 71), 0),
        "page_table": draw_page_table(jax.random.fold_in(keys[13], 71), 0),
        "attn_gain": jnp.clip(1.0 + 0.15 * jax.random.normal(keys[4], (D,), jnp.float32), 0.25, 1.75),
        "w_query": scatter_about(keys[5], (D, INNER), (D * HEAD_DIM) ** -0.5, 0.015625, ((1, 2),)),
        "w_key": scatter_about(keys[6], (D, INNER), D ** -0.5, 0.125, ((1, 2),)),
        "w_value": scatter_about(keys[7], (D, INNER), D ** -0.5, 0.125, ((1, 2),)),
        "w_out": noise_with(keys[8], (INNER, D), INNER ** -0.5, 0.1875, ((0, 2),), (0, 1, 2, 2.0)),
        "rel_bias": draw_rel_bias(jax.random.fold_in(keys[13], 71), 0),
        "final_gain": jnp.clip(1.0 + 0.15 * jax.random.normal(keys[10], (D,), jnp.float32), 0.25, 1.75),
        "cross_key": scatter_about(keys[11], (D, INNER), D ** -0.5, 0.125, ((1, 2),)),
        "cross_value": scatter_about(keys[12], (D, INNER), D ** -0.5, 0.125, ((1, 2),)),
    }


epsilon = 1e-06
far_steps = (12, 16, 23, 32, 46, 64, 91)

def buckets(offsets):
    distance = jnp.abs(offsets)
    far_bucket = 8 + sum(((distance >= threshold).astype(jnp.int32) for threshold in far_steps))
    bucket_ids = jnp.where(distance < 8, distance, far_bucket).astype(jnp.int32)
    return bucket_ids + jnp.where(offsets > 0, 16, 0).astype(jnp.int32)

def rms_scale(row_set, gain_row):
    values = row_set.astype(jnp.float32)
    mean_square = lax.optimization_barrier(jnp.mean(values * values, axis=-1, keepdims=True))
    return (values * lax.rsqrt(mean_square + epsilon) * gain_row).astype(jnp.bfloat16)

def attend(queries, keys_local, values_local, segments, rel_bias):
    token_count = queries.shape[0]
    head_count = rel_bias.shape[1]
    head_dim = queries.shape[1] // head_count
    row_block = min(512, token_count)
    query_heads = queries.reshape(token_count, head_count, head_dim).astype(jnp.float32)
    key_heads = keys_local.reshape(token_count, head_count, head_dim).astype(jnp.float32)
    value_heads = values_local.reshape(token_count, head_count, head_dim).astype(jnp.float32)
    positions = jnp.arange(token_count, dtype=jnp.int32)
    bias_table = jnp.transpose(rel_bias)

    def one_block(first_row):
        row_queries = lax.dynamic_slice_in_dim(query_heads, first_row, row_block, 0)
        row_segments = lax.dynamic_slice_in_dim(segments, first_row, row_block, 0)
        scores = jnp.einsum('qhd,khd->hqk', row_queries, key_heads)
        row_positions = first_row + jnp.arange(row_block, dtype=jnp.int32)
        offsets = positions[None, :] - row_positions[:, None]
        bias_tile = jnp.take(bias_table, buckets(offsets), axis=1)
        same_segment = row_segments[:, None] == segments[None, :]
        scores = jnp.where(same_segment[None], scores + bias_tile, -jnp.inf)
        row_max = lax.optimization_barrier(jnp.max(scores, axis=-1, keepdims=True))
        weights = jnp.exp(scores - row_max)
        probabilities = (weights / lax.optimization_barrier(jnp.sum(weights, axis=-1, keepdims=True))).astype(jnp.bfloat16)
        mixed = jnp.einsum('hqk,khd->qhd', probabilities.astype(jnp.float32), value_heads)
        return mixed.astype(jnp.bfloat16)
    block_starts = (jnp.arange(token_count // row_block, dtype=jnp.int32) * row_block).astype(jnp.int32)
    outcome = lax.map(one_block, block_starts)
    return outcome.reshape(token_count, head_count * head_dim)

def reference(arrivals, packing, segment_ids, page_table, attn_gain, w_query, w_key, w_value, w_out, rel_bias, final_gain, cross_key, cross_value):
    token_count, width = arrivals.shape
    block_count = token_count // PAGE
    arrived = arrivals.reshape(block_count, PAGE, width)
    packed = jnp.zeros_like(arrived).at[packing].set(arrived).reshape(token_count, width)
    normed = rms_scale(packed, attn_gain)
    queries = jnp.dot(normed, w_query, preferred_element_type=jnp.float32).astype(jnp.bfloat16)
    keys_all = jnp.dot(normed, w_key, preferred_element_type=jnp.float32).astype(jnp.bfloat16)
    values_all = jnp.dot(normed, w_value, preferred_element_type=jnp.float32).astype(jnp.bfloat16)
    inner_width = w_query.shape[1]

    def per_device(pieces):
        return attend(pieces[0], pieces[1], pieces[2], pieces[3], rel_bias)
    context = lax.map(per_device, (queries.reshape(N_REQ, TOK_DEV, inner_width), keys_all.reshape(N_REQ, TOK_DEV, inner_width), values_all.reshape(N_REQ, TOK_DEV, inner_width), segment_ids.reshape(N_REQ, TOK_DEV))).reshape(token_count, inner_width)
    group_width = inner_width // HEAD_GROUPS

    def add_group(summed, group_index):
        context_group = lax.dynamic_slice_in_dim(context, group_index * group_width, group_width, 1)
        weight_group = lax.dynamic_slice_in_dim(w_out, group_index * group_width, group_width, 0)
        product = jnp.dot(context_group, weight_group, preferred_element_type=jnp.float32).astype(jnp.bfloat16)
        return (summed + lax.optimization_barrier(product).astype(jnp.float32), None)
    attended, unused_rest = lax.scan(add_group, jnp.zeros((token_count, width), jnp.float32), jnp.arange(HEAD_GROUPS, dtype=jnp.int32))
    hidden = (packed.astype(jnp.float32) + attended).astype(jnp.bfloat16)
    final = rms_scale(hidden, final_gain)
    cross_keys = jnp.dot(final, cross_key, preferred_element_type=jnp.float32).astype(jnp.bfloat16)
    cross_values = jnp.dot(final, cross_value, preferred_element_type=jnp.float32).astype(jnp.bfloat16)
    pages = jnp.stack([cross_keys, cross_values], axis=1).reshape(block_count, PAGE, 2, inner_width)
    cache = jnp.zeros_like(pages).at[page_table].set(pages)
    return (hidden, cache)
```

```python
import numpy as np
import jax
import jax.numpy as jnp
from jax import lax
from jax.experimental import pallas as pl
from jax.experimental.pallas import tpu as pltpu
from jax.sharding import PartitionSpec as P

PAGE = 128
LANES = 4
EPS = 1e-06
FAR_STEPS = (12, 16, 23, 32, 46, 64, 91)
BF = jnp.bfloat16
F32 = jnp.float32


def bucket_one_hot(span, base, bucket_count):
    offsets = np.arange(span) + base
    distance = np.abs(offsets)
    far = 8 + sum((distance >= step).astype(np.int32) for step in FAR_STEPS)
    ids = np.where(distance < 8, distance, far) + np.where(offsets > 0, 16, 0)
    return (np.arange(bucket_count)[:, None] == ids[None, :]).astype(np.float32)


def move(value, m, flip, req_count, tp_count):
    pairs = []
    for r in range(req_count):
        for t in range(tp_count):
            pairs.append((r * tp_count + t, (r ^ m) * tp_count + (t ^ flip)))
    return lax.ppermute(value, ("req", "tp"), pairs)


def pack_kernel(info_ref, gain_ref, *refs):
    owns, others = refs[:LANES], refs[LANES:2 * LANES]
    packed_ref, normed_ref = refs[2 * LANES:]
    half = owns[0].shape[1]
    tp = info_ref[LANES]
    own_at = pl.multiple_of(tp * half, half)
    other_at = pl.multiple_of((1 - tp) * half, half)
    for m in range(LANES):
        row = pl.multiple_of(info_ref[m] * PAGE, PAGE)
        own = owns[m][...].astype(F32)
        other = others[m][...].astype(F32)
        total = jnp.sum(own * own, axis=1, keepdims=True) + jnp.sum(other * other, axis=1, keepdims=True)
        scale = lax.rsqrt(total * (1.0 / (2 * half)) + EPS)
        packed_ref[pl.ds(row, PAGE), pl.ds(own_at, half)] = owns[m][...]
        packed_ref[pl.ds(row, PAGE), pl.ds(other_at, half)] = others[m][...]
        normed_ref[pl.ds(row, PAGE), pl.ds(own_at, half)] = (
            own * scale * gain_ref[:, pl.ds(own_at, half)]).astype(BF)
        normed_ref[pl.ds(row, PAGE), pl.ds(other_at, half)] = (
            other * scale * gain_ref[:, pl.ds(other_at, half)]).astype(BF)


def attend_kernel(normed_ref, wq_ref, wk_ref, wv_ref, table_ref, seg_col_ref, seg_row_ref, ctx_ref,
                  q_ref, k_ref, v_ref, mask_ref, bias_ref):
    tokens = normed_ref.shape[0]
    tiles = tokens // PAGE

    @pl.when(pl.program_id(0) == 0)
    def _():
        mask_ref[...] = jnp.where(seg_col_ref[...] == seg_row_ref[...], 0.0, -1e30)

    normed = normed_ref[...]
    q_ref[...] = jnp.dot(normed, wq_ref[...], preferred_element_type=F32).astype(BF)
    k_ref[...] = jnp.dot(normed, wk_ref[...], preferred_element_type=F32).astype(BF)
    v_ref[...] = jnp.dot(normed, wv_ref[...], preferred_element_type=F32).astype(BF)
    low = lax.broadcasted_iota(jnp.int32, (PAGE, 128), 1) < 64
    span = table_ref.shape[2]
    for pair in range(q_ref.shape[1] // 128):
        cols = slice(pair * 128, pair * 128 + 128)
        for side in range(2):
            base = jnp.broadcast_to(table_ref[0, pair * 2 + side:pair * 2 + side + 1, :], (PAGE, span))
            bias_ref[side] = pltpu.roll(base, 0, 1, stride=1, stride_axis=0)[:, 128:]
        for i in range(tiles):
            first, last = max(0, i - 2), min(tiles - 1, i + 2)
            rows = slice(i * PAGE, i * PAGE + PAGE)
            keys = slice(first * PAGE, last * PAGE + PAGE)
            bias_cols = slice((first - i + 2) * PAGE, (last - i + 3) * PAGE)
            q = q_ref[rows, cols]
            k = k_ref[keys, cols]
            v = v_ref[keys, cols]
            mixed = []
            for side in range(2):
                mine = low if side == 0 else jnp.logical_not(low)
                s = lax.dot_general(jnp.where(mine, q, jnp.zeros_like(q)), k, (((1,), (1,)), ((), ())),
                                    preferred_element_type=F32)
                s = s + bias_ref[side, :, bias_cols] + mask_ref[rows, keys]
                top = jnp.max(s, axis=1, keepdims=True)
                w = jnp.exp(s - top)
                total = jnp.sum(w, axis=1, keepdims=True)
                pv = jnp.dot(w.astype(BF), v, preferred_element_type=F32)
                mixed.append(pv / total)
            ctx_ref[rows, cols] = jnp.where(low, mixed[0], mixed[1]).astype(BF)


def attend_call(normed, w_query, w_key, w_value, table, seg_col, seg_row, first, steps, width):
    tokens, features = normed.shape
    heads = width // 64
    weight = pl.BlockSpec((features, width), lambda g: (0, g + first))
    return pl.pallas_call(
        attend_kernel,
        grid=(steps,),
        in_specs=[
            pl.BlockSpec((tokens, features), lambda g: (0, 0)),
            weight, weight, weight,
            pl.BlockSpec((1, heads, table.shape[2]), lambda g: (g + first, 0, 0)),
            pl.BlockSpec((tokens, 1), lambda g: (0, 0)),
            pl.BlockSpec((1, tokens), lambda g: (0, 0)),
        ],
        out_specs=pl.BlockSpec((tokens, width), lambda g: (0, g)),
        out_shape=jax.ShapeDtypeStruct((tokens, steps * width), BF),
        scratch_shapes=[pltpu.VMEM((tokens, width), BF)] * 3
        + [pltpu.VMEM((tokens, tokens), F32), pltpu.VMEM((2, PAGE, table.shape[2] - 128), F32)],
        name="attend",
    )(normed, w_query, w_key, w_value, table, seg_col, seg_row)


def hidden_kernel(info_ref, packed_ref, ctx_a_ref, ctx_b_ref, oth_a_ref, oth_b_ref, wa_ref, wb_ref, r0_ref, r1_ref,
                  r2_ref, r3_ref, gain_ref, hid_ref, final_ref, all_ref, sq_ref, sel_ref):
    step = pl.program_id(0)
    core, tp = info_ref[0], info_ref[1]
    width = wa_ref.shape[1]
    quarter = r0_ref.shape[0]

    @pl.when(step == 0)
    def _():
        sq_ref[...] = jnp.zeros_like(sq_ref)

    @pl.when((step == 0) & (core == 0))
    def _():
        sel_ref[0] = oth_a_ref[...]
        sel_ref[1] = oth_b_ref[...]

    @pl.when((step == 0) & (core != 0))
    def _():
        sel_ref[0] = oth_b_ref[...]
        sel_ref[1] = oth_a_ref[...]

    mine = jnp.dot(ctx_a_ref[...], wa_ref[...], preferred_element_type=F32)
    mine = mine + jnp.dot(ctx_b_ref[...], wb_ref[...], preferred_element_type=F32)
    theirs = jnp.dot(sel_ref[0, :, :quarter], r0_ref[...], preferred_element_type=F32)
    theirs = theirs + jnp.dot(sel_ref[0, :, quarter:], r1_ref[...], preferred_element_type=F32)
    theirs = theirs + jnp.dot(sel_ref[1, :, :quarter], r2_ref[...], preferred_element_type=F32)
    theirs = theirs + jnp.dot(sel_ref[1, :, quarter:], r3_ref[...], preferred_element_type=F32)
    attended = mine.astype(BF).astype(F32) + theirs.astype(BF).astype(F32)
    hidden = (packed_ref[...].astype(F32) + attended).astype(BF)
    all_ref[step] = hidden
    hidden = hidden.astype(F32)
    sq_ref[...] += jnp.sum(hidden * hidden, axis=1, keepdims=True)
    half_steps = pl.num_programs(0) // 2

    @pl.when(step // half_steps == tp)
    def _():
        hid_ref[...] = all_ref[step]

    @pl.when(step == pl.num_programs(0) - 1)
    def _():
        scale = lax.rsqrt(sq_ref[...] * (1.0 / final_ref.shape[1]) + EPS)
        for j in range(all_ref.shape[0]):
            cols = slice(j * width, j * width + width)
            final_ref[:, cols] = (all_ref[j].astype(F32) * scale * gain_ref[:, cols]).astype(BF)


def hidden_call(info, packed, ctx_a, ctx_b, oth_a, oth_b, w_out, pieces, gain):
    tokens, features = packed.shape
    width = 256
    steps = features // width
    part = ctx_a.shape[1]
    whole = lambda j, info: (0, 0)
    tile = lambda j, info: (0, j)
    ctx_spec = pl.BlockSpec((tokens, part), whole)
    piece_spec = pl.BlockSpec((pieces[0].shape[0], width), tile)
    half_steps = steps // 2
    return pl.pallas_call(
        hidden_kernel,
        grid_spec=pltpu.PrefetchScalarGridSpec(
            num_scalar_prefetch=1,
            grid=(steps,),
            in_specs=[
                pl.BlockSpec((tokens, width), tile),
                ctx_spec, ctx_spec, ctx_spec, ctx_spec,
                pl.BlockSpec((part, width), lambda j, info: (0, j)),
                pl.BlockSpec((part, width), lambda j, info: (1, j)),
                piece_spec, piece_spec, piece_spec, piece_spec,
                pl.BlockSpec((1, features), whole),
            ],
            out_specs=[
                pl.BlockSpec((tokens, width),
                             lambda j, info: (0, jnp.clip(j - info[1] * half_steps, 0, half_steps - 1))),
                pl.BlockSpec((tokens, features), whole),
            ],
            scratch_shapes=[pltpu.VMEM((steps, tokens, width), BF), pltpu.VMEM((tokens, 1), F32),
                            pltpu.VMEM((2, tokens, part), BF)],
        ),
        out_shape=[jax.ShapeDtypeStruct((tokens, features // 2), BF),
                   jax.ShapeDtypeStruct((tokens, features), BF)],
        name="hidden",
    )(info, packed, ctx_a, ctx_b, oth_a, oth_b, w_out, w_out, *pieces, gain)


def cross_kernel(info_ref, first_ref, second_ref, k0_ref, k1_ref, v0_ref, v1_ref, *refs):
    out_ref = refs[-1]
    first, second = first_ref[0], second_ref[0]
    keys = jnp.dot(first, k0_ref[...], preferred_element_type=F32)
    keys = keys + jnp.dot(second, k1_ref[...], preferred_element_type=F32)
    values = jnp.dot(first, v0_ref[...], preferred_element_type=F32)
    values = values + jnp.dot(second, v1_ref[...], preferred_element_type=F32)
    out_ref[0] = jnp.stack([keys, values], axis=1).astype(BF)


def cross_call(info, first, second, cross_key, cross_value, blocks, cache=None):
    lanes, page, half = first.shape
    width = 256
    columns = cross_key.shape[1]
    rows_spec = pl.BlockSpec((1, page, half), lambda j, m, info: (m, 0, 0))
    half_a = pl.BlockSpec((half, width), lambda j, m, info: (info[lanes], j))
    half_b = pl.BlockSpec((half, width), lambda j, m, info: (info[lanes + 1], j))
    extra = [] if cache is None else [cache]
    return pl.pallas_call(
        cross_kernel,
        grid_spec=pltpu.PrefetchScalarGridSpec(
            num_scalar_prefetch=1,
            grid=(columns // width, lanes),
            in_specs=[rows_spec, rows_spec, half_a, half_b, half_a, half_b]
            + [pl.BlockSpec(memory_space=pl.ANY)] * len(extra),
            out_specs=pl.BlockSpec((1, page, 2, width), lambda j, m, info: (info[m], 0, 0, j)),
        ),
        out_shape=jax.ShapeDtypeStruct((blocks, page, 2, columns), BF),
        input_output_aliases={7: 0} if extra else {},
        name="cross",
    )(info, first, second, cross_key, cross_key, cross_value, cross_value, *extra)


def shards(arrivals, packing, segment_ids, page_table, attn_gain, w_query, w_key, w_value, w_out, rel_bias,
           final_gain, cross_key, cross_value):
    req_count, tp_count = lax.axis_size("req"), lax.axis_size("tp")
    r, t = lax.axis_index("req"), lax.axis_index("tp")
    core = r & 1
    tokens, half = arrivals.shape
    blocks = tokens // PAGE

    def go(value, m, flip):
        return move(value, m, flip, req_count, tp_count)

    def place(entries, owner):
        hit = entries // LANES == owner
        return jnp.sum(jnp.where(hit, jnp.arange(LANES, dtype=jnp.int32), 0)), jnp.sum(
            jnp.where(hit, entries % LANES, 0))

    tags = jnp.concatenate([packing, page_table])
    all_tags = [tags] + [go(tags, m, 0) for m in range(1, LANES)]
    slots = [place(all_tags[m][:LANES], r)[1] for m in range(LANES)]
    page_slots = [place(all_tags[m][LANES:], r)[1] for m in range(LANES)]
    outgoing = [lax.dynamic_slice_in_dim(arrivals, place(packing, r ^ m)[0] * PAGE, PAGE, 0) for m in range(LANES)]
    sent_pages = [place(page_table, r ^ m)[0] for m in range(LANES)]

    far2 = go(outgoing[2], 2, 1)
    far3 = go(outgoing[3], 3, 1)
    other0 = go(outgoing[0], 0, 1)
    other1 = go(outgoing[1], 1, 1)
    own1 = go(outgoing[1], 1, 0)
    own2 = go(far2, 0, 1)
    own3 = go(far3, 0, 1)

    one_hot = jnp.asarray(bucket_one_hot(6 * PAGE, -3 * PAGE, rel_bias.shape[0]))
    table = jnp.dot(jnp.transpose(rel_bias), one_hot, precision=lax.Precision.HIGHEST)
    table = table.reshape(4, table.shape[0] // 4, 6 * PAGE)

    whole = pl.BlockSpec(memory_space=pltpu.VMEM)
    packed, normed = pl.pallas_call(
        pack_kernel,
        in_specs=[pl.BlockSpec(memory_space=pltpu.SMEM)] + [whole] * (2 * LANES + 1),
        out_specs=[whole, whole],
        out_shape=[jax.ShapeDtypeStruct((tokens, 2 * half), BF)] * 2,
        name="pack",
    )(jnp.stack(slots + [t]), attn_gain[None, :], outgoing[0], own1, own2, own3, other0, other1, far2, far3)

    quarter = w_out.shape[0] // 4
    near_w = lax.dynamic_slice_in_dim(w_out, core * (2 * quarter), quarter, 0)
    far_w = lax.dynamic_slice_in_dim(w_out, core * (2 * quarter) + quarter, quarter, 0)
    near_w, far_w, _, _ = lax.optimization_barrier((near_w, far_w, own2, own3))
    r0 = go(near_w, 0, 1)
    r1 = go(far_w, 2, 1)
    r2 = go(r0, 1, 0)
    r3 = go(r1, 1, 0)

    seg_col, seg_row = segment_ids[:, None], segment_ids[None, :]
    ctx_a = attend_call(normed, w_query, w_key, w_value, table, seg_col, seg_row, 0, 2, 256)
    oth_a = go(ctx_a, 0, 1)
    ctx_b = attend_call(normed, w_query, w_key, w_value, table, seg_col, seg_row, 2, 2, 256)
    oth_b = go(ctx_b, 0, 1)

    hidden_out, final = hidden_call(jnp.stack([core, t]), packed, ctx_a, ctx_b, oth_a, oth_b, w_out,
                                    (r0, r1, r2, r3), final_gain[None, :])

    def final_half(m):
        return lax.dynamic_slice(final, (sent_pages[m] * PAGE, t * half), (PAGE, half))

    def final_rows(m):
        return lax.dynamic_slice_in_dim(final, sent_pages[m] * PAGE, PAGE, 0)

    page_far2 = go(final_half(2), 2, 1)
    page_own2 = go(page_far2, 0, 1)
    page_far3 = go(final_half(3), 3, 1)
    page_own3 = go(page_far3, 0, 1)
    near = jnp.stack([final_rows(0), go(final_rows(1), 1, 0)])
    zero = jnp.int32(0)
    cache = cross_call(jnp.stack([page_slots[0], page_slots[1], zero, zero + 1]), near[:, :, :half],
                       near[:, :, half:], cross_key, cross_value, blocks)
    cache = cross_call(jnp.stack([page_slots[2], page_slots[3], t, 1 - t]), jnp.stack([page_own2, page_own3]),
                       jnp.stack([page_far2, page_far3]), cross_key, cross_value, blocks, cache)
    return hidden_out, cache


def solution(mesh):
    return jax.shard_map(
        shards,
        mesh=mesh,
        in_specs=(P("req", "tp"), P("req"), P("req"), P("req"), P(), P(None, "tp"), P(None, "tp"), P(None, "tp"),
                  P("tp", None), P(None, "tp"), P(), P(None, "tp"), P(None, "tp")),
        out_specs=(P("req", "tp"), P("req", None, None, "tp")),
        check_vma=False,
    )
```
